512 devices in a mesh: hst: 128 (over z, y, core), local: 4 (over x).
Axes of the slice: x: 4, y: 8, z: 8, core: 2. Of those that a mesh axis runs over, the one named last changes fastest.
Arguments:
- grads: bfloat16 [128, 4, 16, 49152], P('hst', 'local'), may hold values from -1.25 to 1.25
- master: float32 [16, 49152], P('local', 'hst'), may hold values from -3 to 3
- moment_one: float32 [16, 49152], P('local', 'hst'), may hold values from -3 to 3
- moment_two: float32 [16, 49152], P('local', 'hst'), may hold values from 0.01 to 2
Outputs:
- grad_total: float32 [16, 49152], P('local', 'hst')
- new_master: float32 [16, 49152], P('local', 'hst')
- new_one: float32 [16, 49152], P('local', 'hst')
- new_two: float32 [16, 49152], P('local', 'hst')
- secondary: bfloat16 [16, 49152], P('local')
The draws below stay inside these ranges and needn't reach their ends.
All inputs are finite; a program needn't handle non-finite values.
Results may differ from the reference program's by a relative error of at most 0.001.
Values may be sent and summed in bfloat16 or wider, within the bound.
A program may use at most 64 MiB of HBM per device.

```python
import math
import jax
import jax.numpy as jnp
from jax import lax

COLS = 49152
ROWS = 16
N_HST = 128
N_LOCAL = 4


def spiked(result, key, source, target, blocks, factor):
    def block_of(position):
        return (jnp.arange(result.shape[position]) // (result.shape[position] // blocks)).reshape((-1,) + (1,) * (result.ndim - 1 - position))

    one_side = jax.random.permutation(key, blocks)[block_of(target)]
    other_side = (block_of(target) + blocks // 2) % blocks
    return jnp.where((block_of(source) == one_side) | (block_of(source) == other_side), factor * result, result)


def level_of(rng, extent, cuts, low, largest):
    level, own = 1.0, jax.random.fold_in(rng, 6)
    for dim, shards_of in cuts:
        heights = jnp.exp(jax.random.uniform(jax.random.fold_in(own, dim), (shards_of,), jnp.float32, low / len(cuts), largest / len(cuts)))
        level = level * jnp.repeat(heights, extent[dim] // shards_of).reshape([-1 if axis == dim else 1 for axis in range(len(extent))])
    return level


def bell_draw(key, dims, deviation, most, shards=(), dtype=jnp.bfloat16):
    array = jax.random.normal(key, dims, jnp.float32) * deviation
    if len(shards) > 0:
        array = level_of(key, dims, shards, -0.22, 0.18) * array
    return jnp.clip(array, min=-most, max=most).astype(dtype)


def bell_draw_with(rng, extent, deviation, limit, cuts, heavy, held_as=jnp.bfloat16):
    array = deviation * jax.random.normal(rng, extent, jnp.float32)
    if cuts:
        array = array * level_of(rng, extent, cuts, -0.22, 0.18)
    return jnp.clip(spiked(array, jax.random.fold_in(rng, 3), *heavy), -limit, limit).astype(held_as)


def setup_inputs(seed: int = 0) -> dict:
    seeds = jax.random.split(jax.random.key(seed), 5)
    return {
        "grads": bell_draw_with(seeds[0], (N_HST, N_LOCAL, ROWS, COLS), 0.05, 1.25, ((0, 128), (1, 4)), (0, 3, 128, 5.5)),
        "master": bell_draw(seeds[1], (ROWS, COLS), 0.5, 3.0, ((0, 4), (1, 128)), jnp.float32),
        "moment_one": bell_draw(seeds[2], (ROWS, COLS), 0.5, 3.0, ((0, 4), (1, 128)), jnp.float32),
        "moment_two": jnp.clip(jnp.exp(math.log(2.0) - 5.2983174 * jax.random.uniform(seeds[3], (ROWS, COLS), jnp.float32) ** level_of(seeds[3], (ROWS, COLS), ((0, 4), (1, 128)), -0.2, 0.2)), 0.01, 2.0),
    }


beta_one = 0.9
beta_two = 0.95
learn_rate = 0.02
decay_rate = 0.1
epsilon = 1e-08
correct_one = 1.0 - (0.9 ** 50) ** 2
correct_two = 1.0 - (0.95 ** 50) ** 2

def reference(grads, master, moment_one, moment_two):
    grad_total = lax.optimization_barrier(jnp.sum(grads.astype(jnp.float32), axis=(0, 1)))
    new_one = beta_one * moment_one + (1.0 - beta_one) * grad_total
    new_two = beta_two * moment_two + (1.0 - beta_two) * grad_total * grad_total
    update = new_one / correct_one / (jnp.sqrt(new_two / correct_two) + epsilon)
    new_master = master - learn_rate * (update + decay_rate * master)
    return (grad_total, new_master, new_one, new_two, new_master.astype(jnp.bfloat16))
```

```python
import functools

import jax
import jax.numpy as jnp
from jax import lax
from jax.experimental import pallas as pl
from jax.experimental.pallas import tpu as pltpu
from jax.sharding import PartitionSpec as P

beta_one = 0.9
beta_two = 0.95
learn_rate = 0.02
decay_rate = 0.1
epsilon = 1e-08
correct_one = 1.0 - (0.9**50) ** 2
correct_two = 1.0 - (0.95**50) ** 2

NX, NY, NZ, NC = 4, 8, 8, 2
PARTS, LANES = 3, 128
MESH = pl.DeviceIdType.MESH
SEMS = 101


def kernel(
    grads,
    master,
    moment_one,
    moment_two,
    total_out,
    master_out,
    one_out,
    two_out,
    gathered,
    own,
    peer,
    sum_z,
    sum_y,
    sum_x,
    half_z,
    full_z,
    half_y,
    full_y,
    half_x,
    full_x,
    mid_z,
    mid_y,
    mid_x,
    got_z,
    got_y,
    got_x,
    end_z,
    end_y,
    end_x,
    last_z,
    last_y,
    last_x,
    load_sem,
    send_sem,
    recv_sem,
):
    x = lax.axis_index("local")
    h = lax.axis_index("hst")
    z, y, c = h // (NY * NC), (h // NC) % NY, h % NC

    def device(dx=0, dy=0, dz=0, dc=0):
        there = (((z + dz) % NZ) * NY + (y + dy) % NY) * NC + (c + dc) % NC
        return {"hst": there, "local": (x + dx) % NX}

    taken = []

    def send(src, dst, to):
        slot = len(taken)
        copy = pltpu.make_async_remote_copy(
            src_ref=src,
            dst_ref=dst,
            send_sem=send_sem.at[slot],
            recv_sem=recv_sem.at[slot],
            device_id=to,
            device_id_type=MESH,
        )
        copy.start()
        taken.append(copy)
        return copy

    barrier = pltpu.get_barrier_semaphore()
    peers = [device(dc=1)]
    peers += [device(dx=k) for k in range(1, NX)]
    peers += [device(dy=k) for k in range(1, NY)]
    peers += [device(dz=k) for k in range(1, NZ)]
    for to in peers:
        pl.semaphore_signal(barrier, inc=1, device_id=to, device_id_type=MESH)
    loads = []
    for p in range(PARTS):
        load = pltpu.make_async_copy(
            grads.at[:, :, :, c, p], own.at[p], load_sem.at[p]
        )
        load.start()
        loads.append(load)
    pl.semaphore_wait(barrier, len(peers))

    pairs = [
        send(grads.at[:, :, :, 1 - c, p], peer.at[p], device(dc=1))
        for p in range(PARTS)
    ]

    def pair_sum(p, row, i, j):
        return own[p, row, i, j].astype(jnp.float32) + peer[p, row, i, j].astype(
            jnp.float32
        )

    def fill_z(i, carry):
        for j in range(NY):
            for row in range(2):
                sum_z[i, j, row] = pair_sum(0, row, i, j)
        return carry

    def fill_y(i, carry):
        for j in range(NY):
            for row in range(2):
                sum_y[j, i, row] = pair_sum(1, row, i, j)
        return carry

    def fill_x(i, carry):
        for j in range(NY):
            for row in range(2):
                both = pair_sum(2, row, i, j)
                sum_x[2 * row, i, j] = both[0:4]
                sum_x[2 * row + 1, i, j] = both[4:8]
        return carry

    class Ring:
        def __init__(self, sums, half, full, at, size, hop):
            self.sums, self.half, self.full = sums, half, full
            self.at, self.size, self.hop = at, size, hop
            self.flight = [None, None]

        def step(self, s):
            far = self.size // 2
            cut = self.sums.shape[1] // 2
            for way, sign in enumerate((1, -1)):
                to = self.hop(sign)
                chunk = (self.at + self.size + sign * (far - s)) % self.size
                lo = way * cut
                if s == 0:
                    self.flight[way] = send(
                        self.sums.at[chunk, pl.ds(lo, cut)], self.half.at[way], to
                    )
                    continue
                self.flight[way].wait_recv()
                if s == 1:
                    self.sums[chunk, pl.ds(lo, cut)] += self.half[way]
                else:
                    self.sums[chunk] += self.full[way, s - 2]
                self.flight[way] = send(
                    self.sums.at[chunk], self.full.at[way, s - 1], to
                )

        def finish(self):
            for copy in self.flight:
                copy.wait_recv()
            last = self.size // 2 - 2
            return self.sums[self.at] + self.full[0, last] + self.full[1, last]

    ring_z = Ring(sum_z, half_z, full_z, z, NZ, lambda d: device(dz=d + NZ))
    ring_y = Ring(sum_y, half_y, full_y, y, NY, lambda d: device(dy=d + NY))
    ring_x = Ring(sum_x, half_x, full_x, x, NX, lambda d: device(dx=d + NX))

    def spread(part, got, at, size, hop):
        order = sorted(range(1, size), key=lambda k: -min(k, size - k))
        return [
            send(part.at[(at + k) % size], got.at[k - 1], hop(k)) for k in order
        ]

    def collect(copies, part, got, at, size):
        for copy in copies:
            copy.wait_recv()
        total = part[at]
        for k in range(size - 1):
            total = total + got[k]
        return total

    fills = (fill_z, fill_y, fill_x)
    for p, ring in enumerate((ring_z, ring_y, ring_x)):
        loads[p].wait()
        pairs[p].wait_recv()
        lax.fori_loop(0, NZ, fills[p], 0)
        ring.step(0)
    ring_z.step(1)
    ring_y.step(1)
    ring_x.step(1)
    ring_z.step(2)
    ring_y.step(2)
    mid_x[...] = ring_x.finish()
    second_x = spread(mid_x, got_x, z, NZ, lambda k: device(dz=k))
    ring_z.step(3)
    ring_y.step(3)
    mid_z[...] = ring_z.finish()
    second_z = spread(mid_z, got_z, y, NY, lambda k: device(dy=k))
    done_y = ring_y.finish()
    for k in range(NX):
        mid_y[k] = done_y[:, k // 2, (k % 2) * 4 : (k % 2) * 4 + 4]
    second_y = spread(mid_y, got_y, x, NX, lambda k: device(dx=k))

    end_x[...] = collect(second_x, mid_x, got_x, z, NZ)
    third_x = spread(end_x, last_x, y, NY, lambda k: device(dy=k))
    end_y[...] = collect(second_y, mid_y, got_y, x, NX)
    third_y = spread(end_y, last_y, z, NZ, lambda k: device(dz=k))
    done_z = collect(second_z, mid_z, got_z, y, NY)
    for k in range(NX):
        end_z[k] = done_z[k // 2, (k % 2) * 4 : (k % 2) * 4 + 4]
    third_z = spread(end_z, last_z, x, NX, lambda k: device(dx=k))

    thirds = (
        (third_z, end_z, last_z, x, NX),
        (third_y, end_y, last_y, z, NZ),
        (third_x, end_x, last_x, y, NY),
    )
    for p, third in enumerate(thirds):
        columns = pl.ds(p * LANES, LANES)
        grad_total = collect(*third)
        new_one = beta_one * moment_one[:, columns] + (1.0 - beta_one) * grad_total
        new_two = (
            beta_two * moment_two[:, columns]
            + (1.0 - beta_two) * grad_total * grad_total
        )
        update = new_one / correct_one / (jnp.sqrt(new_two / correct_two) + epsilon)
        old = master[:, columns]
        new_master = old - learn_rate * (update + decay_rate * old)
        total_out[:, columns] = grad_total
        master_out[:, columns] = new_master
        one_out[:, columns] = new_one
        two_out[:, columns] = new_two
        gathered[z, y, c, p] = new_master.astype(jnp.bfloat16)

    far_first = (4, 3, 5, 2, 6, 1, 7)
    other = device(dc=1)
    mine = gathered.at[z, y, c, 0]
    first_z = [send(mine, mine, device(dz=k)) for k in far_first]
    mine = gathered.at[z, y, c, pl.ds(1, 2)]
    first_y = [send(mine, mine, device(dy=k)) for k in far_first]

    def arrived(copy):
        copy.wait_recv()

    for copy in first_z:
        arrived(copy)
    line = gathered.at[:, y, c, 0]
    next_y = [send(line, line, device(dy=k)) for k in far_first]
    send(line, line, other)
    for copy in first_y:
        arrived(copy)
    line = gathered.at[z, :, c, pl.ds(1, 2)]
    next_z = [send(line, line, device(dz=k)) for k in far_first]
    send(line, line, other)
    last = len(taken)
    for k, copy in reversed(list(zip(far_first, next_y))):
        arrived(copy)
        line = gathered.at[:, (y + NY - k) % NY, c, 0]
        send(line, line, other)
    for k, copy in reversed(list(zip(far_first, next_z))):
        arrived(copy)
        line = gathered.at[(z + NZ - k) % NZ, :, c, pl.ds(1, 2)]
        send(line, line, other)
    for copy in taken[last - 1 :] + [taken[last - 1 - len(far_first) - 1]]:
        arrived(copy)
    for copy in taken:
        copy.wait_send()
    assert len(taken) == SEMS, len(taken)


def local(grads, master, moment_one, moment_two):
    view = grads.reshape(2, 8, NZ, NY, NC, PARTS, LANES).transpose(0, 2, 3, 4, 5, 1, 6)
    f32, bf16 = jnp.float32, jnp.bfloat16
    block = jax.ShapeDtypeStruct(master.shape, f32)
    vmem = pl.BlockSpec(memory_space=pltpu.VMEM)
    outs = pl.pallas_call(
        kernel,
        out_shape=(block,) * 4
        + (jax.ShapeDtypeStruct((NZ, NY, NC, PARTS, 4, LANES), bf16),),
        in_specs=[pl.BlockSpec(memory_space=pl.ANY), vmem, vmem, vmem],
        out_specs=(vmem,) * 5,
        scratch_shapes=[
            pltpu.VMEM((PARTS, 2, NZ, NY, 8, LANES), bf16),
            pltpu.VMEM((PARTS, 2, NZ, NY, 8, LANES), bf16),
            pltpu.VMEM((NZ, NY, 2, 8, LANES), f32),
            pltpu.VMEM((NY, NZ, 2, 8, LANES), f32),
            pltpu.VMEM((NX, NZ, NY, 4, LANES), f32),
            pltpu.VMEM((2, NY // 2, 2, 8, LANES), f32),
            pltpu.VMEM((2, NZ // 2 - 1, NY, 2, 8, LANES), f32),
            pltpu.VMEM((2, NZ // 2, 2, 8, LANES), f32),
            pltpu.VMEM((2, NY // 2 - 1, NZ, 2, 8, LANES), f32),
            pltpu.VMEM((2, NZ // 2, NY, 4, LANES), f32),
            pltpu.VMEM((2, NX // 2 - 1, NZ, NY, 4, LANES), f32),
            pltpu.VMEM((NY, 2, 8, LANES), f32),
            pltpu.VMEM((NX, NZ, 4, LANES), f32),
            pltpu.VMEM((NZ, NY, 4, LANES), f32),
            pltpu.VMEM((NY - 1, 2, 8, LANES), f32),
            pltpu.VMEM((NX - 1, NZ, 4, LANES), f32),
            pltpu.VMEM((NZ - 1, NY, 4, LANES), f32),
            pltpu.VMEM((NX, 4, LANES), f32),
            pltpu.VMEM((NZ, 4, LANES), f32),
            pltpu.VMEM((NY, 4, LANES), f32),
            pltpu.VMEM((NX - 1, 4, LANES), f32),
            pltpu.VMEM((NZ - 1, 4, LANES), f32),
            pltpu.VMEM((NY - 1, 4, LANES), f32),
            pltpu.SemaphoreType.DMA((PARTS,)),
            pltpu.SemaphoreType.DMA((SEMS,)),
            pltpu.SemaphoreType.DMA((SEMS,)),
        ],
        compiler_params=pltpu.CompilerParams(collective_id=0, has_side_effects=True),
    )(view, master, moment_one, moment_two)
    secondary = outs[4].transpose(4, 0, 1, 2, 3, 5).reshape(master.shape[0], -1)
    return (*outs[:4], secondary)


def solution(mesh):
    return jax.shard_map(
        local,
        mesh=mesh,
        in_specs=(
            P("hst", "local", None, None),
            P("local", "hst"),
            P("local", "hst"),
            P("local", "hst"),
        ),
        out_specs=(
            P("local", "hst"),
            P("local", "hst"),
            P("local", "hst"),
            P("local", "hst"),
            P("local", None),
        ),
        check_vma=False,
    )
```

```python
import functools

import jax
import jax.numpy as jnp
from jax import lax
from jax.experimental import pallas as pl
from jax.experimental.pallas import tpu as pltpu
from jax.sharding import PartitionSpec as P

beta_one = 0.9
beta_two = 0.95
learn_rate = 0.02
decay_rate = 0.1
epsilon = 1e-08
correct_one = 1.0 - (0.9**50) ** 2
correct_two = 1.0 - (0.95**50) ** 2

NX, NY, NZ, NC = 4, 8, 8, 2
PARTS, LANES = 3, 128
MESH = pl.DeviceIdType.MESH
SEMS = 101


def kernel(
    grads,
    master,
    moment_one,
    moment_two,
    packed_out,
    gathered,
    states,
    packed,
    own,
    peer,
    sum_z,
    sum_y,
    sum_x,
    half_z,
    full_z,
    half_y,
    full_y,
    half_x,
    full_x,
    mid_z,
    mid_y,
    mid_x,
    got_z,
    got_y,
    got_x,
    end_z,
    end_y,
    end_x,
    last_z,
    last_y,
    last_x,
    state_sem,
    pack_sem,
    load_sem,
    send_sem,
    recv_sem,
):
    x = lax.axis_index("local")
    h = lax.axis_index("hst")
    z, y, c = h // (NY * NC), (h // NC) % NY, h % NC

    def device(dx=0, dy=0, dz=0, dc=0):
        there = (((z + dz) % NZ) * NY + (y + dy) % NY) * NC + (c + dc) % NC
        return {"hst": there, "local": (x + dx) % NX}

    taken = []

    def send(src, dst, to):
        slot = len(taken)
        copy = pltpu.make_async_remote_copy(
            src_ref=src,
            dst_ref=dst,
            send_sem=send_sem.at[slot],
            recv_sem=recv_sem.at[slot],
            device_id=to,
            device_id_type=MESH,
        )
        copy.start()
        taken.append(copy)
        return copy

    barrier = pltpu.get_barrier_semaphore()
    peers = [device(dc=1)]
    peers += [device(dx=k) for k in range(1, NX)]
    peers += [device(dy=k) for k in range(1, NY)]
    peers += [device(dz=k) for k in range(1, NZ)]
    for to in peers:
        pl.semaphore_signal(barrier, inc=1, device_id=to, device_id_type=MESH)
    loads = []
    for p in range(PARTS):
        load = pltpu.make_async_copy(
            grads.at[:, :, :, c, p], own.at[p], load_sem.at[p]
        )
        load.start()
        loads.append(load)
    state_loads = []
    for k, ref in enumerate((master, moment_one, moment_two)):
        load = pltpu.make_async_copy(ref, states.at[k], state_sem.at[k])
        load.start()
        state_loads.append(load)
    pl.semaphore_wait(barrier, len(peers))

    pairs = [
        send(grads.at[:, :, :, 1 - c, p], peer.at[p], device(dc=1))
        for p in range(PARTS)
    ]

    def pair_sum(p, row, i, j):
        return own[p, row, i, j].astype(jnp.float32) + peer[p, row, i, j].astype(
            jnp.float32
        )

    def fill_z(i, carry):
        for j in range(NY):
            for row in range(2):
                sum_z[i, j, row] = pair_sum(0, row, i, j)
        return carry

    def fill_y(i, carry):
        for j in range(NY):
            for row in range(2):
                sum_y[j, i, row] = pair_sum(1, row, i, j)
        return carry

    def fill_x(i, carry):
        for j in range(NY):
            for row in range(2):
                both = pair_sum(2, row, i, j)
                sum_x[2 * row, i, j] = both[0:4]
                sum_x[2 * row + 1, i, j] = both[4:8]
        return carry

    class Ring:
        def __init__(self, sums, half, full, at, size, hop):
            self.sums, self.half, self.full = sums, half, full
            self.at, self.size, self.hop = at, size, hop
            self.flight = [None, None]

        def step(self, s):
            far = self.size // 2
            cut = self.sums.shape[1] // 2
            for way, sign in enumerate((1, -1)):
                to = self.hop(sign)
                chunk = (self.at + self.size + sign * (far - s)) % self.size
                lo = way * cut
                if s == 0:
                    self.flight[way] = send(
                        self.sums.at[chunk, pl.ds(lo, cut)], self.half.at[way], to
                    )
                    continue
                self.flight[way].wait_recv()
                if s == 1:
                    self.sums[chunk, pl.ds(lo, cut)] += self.half[way]
                else:
                    self.sums[chunk] += self.full[way, s - 2]
                self.flight[way] = send(
                    self.sums.at[chunk], self.full.at[way, s - 1], to
                )

        def finish(self):
            for copy in self.flight:
                copy.wait_recv()
            last = self.size // 2 - 2
            return self.sums[self.at] + self.full[0, last] + self.full[1, last]

    ring_z = Ring(sum_z, half_z, full_z, z, NZ, lambda d: device(dz=d + NZ))
    ring_y = Ring(sum_y, half_y, full_y, y, NY, lambda d: device(dy=d + NY))
    ring_x = Ring(sum_x, half_x, full_x, x, NX, lambda d: device(dx=d + NX))

    def spread(part, got, at, size, hop):
        order = sorted(range(1, size), key=lambda k: -min(k, size - k))
        return [
            send(part.at[(at + k) % size], got.at[k - 1], hop(k)) for k in order
        ]

    def collect(copies, part, got, at, size):
        for copy in copies:
            copy.wait_recv()
        total = part[at]
        for k in range(size - 1):
            total = total + got[k]
        return total

    fills = (fill_z, fill_y, fill_x)
    for p, ring in enumerate((ring_z, ring_y, ring_x)):
        loads[p].wait()
        pairs[p].wait_recv()
        lax.fori_loop(0, NZ, fills[p], 0)
        ring.step(0)
    ring_z.step(1)
    ring_y.step(1)
    ring_x.step(1)
    ring_z.step(2)
    ring_y.step(2)
    mid_x[...] = ring_x.finish()
    second_x = spread(mid_x, got_x, z, NZ, lambda k: device(dz=k))
    ring_z.step(3)
    ring_y.step(3)
    mid_z[...] = ring_z.finish()
    second_z = spread(mid_z, got_z, y, NY, lambda k: device(dy=k))
    done_y = ring_y.finish()
    for k in range(NX):
        mid_y[k] = done_y[:, k // 2, (k % 2) * 4 : (k % 2) * 4 + 4]
    second_y = spread(mid_y, got_y, x, NX, lambda k: device(dx=k))

    end_x[...] = collect(second_x, mid_x, got_x, z, NZ)
    third_x = spread(end_x, last_x, y, NY, lambda k: device(dy=k))
    end_y[...] = collect(second_y, mid_y, got_y, x, NX)
    third_y = spread(end_y, last_y, z, NZ, lambda k: device(dz=k))
    done_z = collect(second_z, mid_z, got_z, y, NY)
    for k in range(NX):
        end_z[k] = done_z[k // 2, (k % 2) * 4 : (k % 2) * 4 + 4]
    third_z = spread(end_z, last_z, x, NX, lambda k: device(dx=k))

    thirds = (
        (third_z, end_z, last_z, x, NX),
        (third_y, end_y, last_y, z, NZ),
        (third_x, end_x, last_x, y, NY),
    )
    for load in state_loads:
        load.wait()
    for p, third in enumerate(thirds):
        columns = pl.ds(p * LANES, LANES)
        grad_total = collect(*third)
        new_one = beta_one * states[1, :, columns] + (1.0 - beta_one) * grad_total
        new_two = (
            beta_two * states[2, :, columns]
            + (1.0 - beta_two) * grad_total * grad_total
        )
        update = new_one / correct_one / (jnp.sqrt(new_two / correct_two) + epsilon)
        old = states[0, :, columns]
        new_master = old - learn_rate * (update + decay_rate * old)
        packed[0, :, columns] = grad_total
        packed[1, :, columns] = new_master
        packed[2, :, columns] = new_one
        packed[3, :, columns] = new_two
        gathered[z, y, c, p] = new_master.astype(jnp.bfloat16)

    far_first = (4, 3, 5, 2, 6, 1, 7)
    other = device(dc=1)
    mine = gathered.at[z, y, c, 0]
    first_z = [send(mine, mine, device(dz=k)) for k in far_first]
    mine = gathered.at[z, y, c, pl.ds(1, 2)]
    first_y = [send(mine, mine, device(dy=k)) for k in far_first]

    pack = pltpu.make_async_copy(packed, packed_out, pack_sem)
    pack.start()

    def arrived(copy):
        copy.wait_recv()

    for copy in first_z:
        arrived(copy)
    line = gathered.at[:, y, c, 0]
    next_y = [send(line, line, device(dy=k)) for k in far_first]
    send(line, line, other)
    for copy in first_y:
        arrived(copy)
    line = gathered.at[z, :, c, pl.ds(1, 2)]
    next_z = [send(line, line, device(dz=k)) for k in far_first]
    send(line, line, other)
    last = len(taken)
    for k, copy in reversed(list(zip(far_first, next_y))):
        arrived(copy)
        line = gathered.at[:, (y + NY - k) % NY, c, 0]
        send(line, line, other)
    for k, copy in reversed(list(zip(far_first, next_z))):
        arrived(copy)
        line = gathered.at[(z + NZ - k) % NZ, :, c, pl.ds(1, 2)]
        send(line, line, other)
    for copy in taken[last - 1 :] + [taken[last - 1 - len(far_first) - 1]]:
        arrived(copy)
    for copy in taken:
        copy.wait_send()
    pack.wait()
    assert len(taken) == SEMS, len(taken)


def finish(packed, gathered, *refs):
    outs, (states, weights, load_sem, store_sem) = refs[:5], refs[5:]
    first = pltpu.make_async_copy(gathered, weights, load_sem.at[0])
    second = pltpu.make_async_copy(packed, states, load_sem.at[1])
    first.start()
    second.start()
    first.wait()
    stores = [pltpu.make_async_copy(weights, outs[4], store_sem.at[4])]
    stores[0].start()
    second.wait()
    for k in range(4):
        store = pltpu.make_async_copy(states.at[k], outs[k], store_sem.at[k])
        store.start()
        stores.append(store)
    for store in stores:
        store.wait()


def local(grads, master, moment_one, moment_two):
    view = grads.reshape(2, 8, NZ, NY, NC, PARTS, LANES).transpose(0, 2, 3, 4, 5, 1, 6)
    f32, bf16 = jnp.float32, jnp.bfloat16
    block = jax.ShapeDtypeStruct(master.shape, f32)
    block_all = jax.ShapeDtypeStruct((4,) + master.shape, f32)
    weights = jax.ShapeDtypeStruct((NZ, NY, NC, PARTS, 4, LANES), bf16)
    vmem = pl.BlockSpec(memory_space=pltpu.VMEM)
    hbm = pl.BlockSpec(memory_space=pl.ANY)
    packed, gathered = pl.pallas_call(
        kernel,
        out_shape=(block_all, weights),
        in_specs=[hbm] * 4,
        out_specs=(hbm, vmem),
        scratch_shapes=[
            pltpu.VMEM((3,) + master.shape, f32),
            pltpu.VMEM((4,) + master.shape, f32),
            pltpu.VMEM((PARTS, 2, NZ, NY, 8, LANES), bf16),
            pltpu.VMEM((PARTS, 2, NZ, NY, 8, LANES), bf16),
            pltpu.VMEM((NZ, NY, 2, 8, LANES), f32),
            pltpu.VMEM((NY, NZ, 2, 8, LANES), f32),
            pltpu.VMEM((NX, NZ, NY, 4, LANES), f32),
            pltpu.VMEM((2, NY // 2, 2, 8, LANES), f32),
            pltpu.VMEM((2, NZ // 2 - 1, NY, 2, 8, LANES), f32),
            pltpu.VMEM((2, NZ // 2, 2, 8, LANES), f32),
            pltpu.VMEM((2, NY // 2 - 1, NZ, 2, 8, LANES), f32),
            pltpu.VMEM((2, NZ // 2, NY, 4, LANES), f32),
            pltpu.VMEM((2, NX // 2 - 1, NZ, NY, 4, LANES), f32),
            pltpu.VMEM((NY, 2, 8, LANES), f32),
            pltpu.VMEM((NX, NZ, 4, LANES), f32),
            pltpu.VMEM((NZ, NY, 4, LANES), f32),
            pltpu.VMEM((NY - 1, 2, 8, LANES), f32),
            pltpu.VMEM((NX - 1, NZ, 4, LANES), f32),
            pltpu.VMEM((NZ - 1, NY, 4, LANES), f32),
            pltpu.VMEM((NX, 4, LANES), f32),
            pltpu.VMEM((NZ, 4, LANES), f32),
            pltpu.VMEM((NY, 4, LANES), f32),
            pltpu.VMEM((NX - 1, 4, LANES), f32),
            pltpu.VMEM((NZ - 1, 4, LANES), f32),
            pltpu.VMEM((NY - 1, 4, LANES), f32),
            pltpu.SemaphoreType.DMA((3,)),
            pltpu.SemaphoreType.DMA,
            pltpu.SemaphoreType.DMA((PARTS,)),
            pltpu.SemaphoreType.DMA((SEMS,)),
            pltpu.SemaphoreType.DMA((SEMS,)),
        ],
        compiler_params=pltpu.CompilerParams(collective_id=0, has_side_effects=True),
    )(view, master, moment_one, moment_two)
    outs = pl.pallas_call(
        finish,
        out_shape=(block,) * 4 + (weights,),
        in_specs=[hbm] * 2,
        out_specs=(hbm,) * 5,
        scratch_shapes=[
            pltpu.VMEM(block_all.shape, f32),
            pltpu.VMEM(weights.shape, bf16),
            pltpu.SemaphoreType.DMA((2,)),
            pltpu.SemaphoreType.DMA((5,)),
        ],
    )(packed, gathered)
    secondary = outs[4].transpose(4, 0, 1, 2, 3, 5).reshape(master.shape[0], -1)
    return (*outs[:4], secondary)


def solution(mesh):
    return jax.shard_map(
        local,
        mesh=mesh,
        in_specs=(
            P("hst", "local", None, None),
            P("local", "hst"),
            P("local", "hst"),
            P("local", "hst"),
        ),
        out_specs=(
            P("local", "hst"),
            P("local", "hst"),
            P("local", "hst"),
            P("local", "hst"),
            P("local", None),
        ),
        check_vma=False,
    )
```

```python
import functools

import jax
import jax.numpy as jnp
from jax import lax
from jax.experimental import pallas as pl
from jax.experimental.pallas import tpu as pltpu
from jax.sharding import PartitionSpec as P

beta_one = 0.9
beta_two = 0.95
learn_rate = 0.02
decay_rate = 0.1
epsilon = 1e-08
correct_one = 1.0 - (0.9**50) ** 2
correct_two = 1.0 - (0.95**50) ** 2

NX, NY, NZ, NC = 4, 8, 8, 2
PARTS, LANES = 3, 128
MESH = pl.DeviceIdType.MESH
SEMS = 101


def kernel(
    grads,
    master,
    moment_one,
    moment_two,
    packed_out,
    gathered,
    states,
    packed,
    own,
    peer,
    sum_z,
    sum_y,
    sum_x,
    half_z,
    full_z,
    half_y,
    full_y,
    half_x,
    full_x,
    mid_z,
    mid_y,
    mid_x,
    got_z,
    got_y,
    got_x,
    end_z,
    end_y,
    end_x,
    last_z,
    last_y,
    last_x,
    state_sem,
    pack_sem,
    load_sem,
    send_sem,
    recv_sem,
):
    x = lax.axis_index("local")
    h = lax.axis_index("hst")
    z, y, c = h // (NY * NC), (h // NC) % NY, h % NC

    def device(dx=0, dy=0, dz=0, dc=0):
        there = (((z + dz) % NZ) * NY + (y + dy) % NY) * NC + (c + dc) % NC
        return {"hst": there, "local": (x + dx) % NX}

    taken = []

    def send(src, dst, to):
        slot = len(taken)
        copy = pltpu.make_async_remote_copy(
            src_ref=src,
            dst_ref=dst,
            send_sem=send_sem.at[slot],
            recv_sem=recv_sem.at[slot],
            device_id=to,
            device_id_type=MESH,
        )
        copy.start()
        taken.append(copy)
        return copy

    barrier = pltpu.get_barrier_semaphore()
    peers = [device(dc=1)]
    peers += [device(dx=k) for k in (1, NX - 1)]
    peers += [device(dy=k) for k in (1, NY - 1)]
    peers += [device(dz=k) for k in (1, NZ - 1)]
    for to in peers:
        pl.semaphore_signal(barrier, inc=1, device_id=to, device_id_type=MESH)
    loads = []
    for p in range(PARTS):
        load = pltpu.make_async_copy(
            grads.at[:, :, :, c, p], own.at[p], load_sem.at[p]
        )
        load.start()
        loads.append(load)
    state_loads = []
    for k, ref in enumerate((master, moment_one, moment_two)):
        load = pltpu.make_async_copy(ref, states.at[k], state_sem.at[k])
        load.start()
        state_loads.append(load)
    pl.semaphore_wait(barrier, len(peers))

    pairs = [
        send(grads.at[:, :, :, 1 - c, p], peer.at[p], device(dc=1))
        for p in range(PARTS)
    ]

    def pair_sum(p, row, i, j):
        return own[p, row, i, j].astype(jnp.float32) + peer[p, row, i, j].astype(
            jnp.float32
        )

    def fill_z(i, carry):
        for j in range(NY):
            for row in range(2):
                sum_z[i, j, row] = pair_sum(0, row, i, j)
        return carry

    def fill_y(i, carry):
        for j in range(NY):
            for row in range(2):
                sum_y[j, i, row] = pair_sum(1, row, i, j)
        return carry

    def fill_x(i, carry):
        for j in range(NY):
            for row in range(2):
                both = pair_sum(2, row, i, j)
                sum_x[2 * row, i, j] = both[0:4]
                sum_x[2 * row + 1, i, j] = both[4:8]
        return carry

    class Ring:
        def __init__(self, sums, half, full, at, size, hop):
            self.sums, self.half, self.full = sums, half, full
            self.at, self.size, self.hop = at, size, hop
            self.flight = [None, None]

        def step(self, s):
            far = self.size // 2
            cut = self.sums.shape[1] // 2
            for way, sign in enumerate((1, -1)):
                to = self.hop(sign)
                chunk = (self.at + self.size + sign * (far - s)) % self.size
                lo = way * cut
                if s == 0:
                    self.flight[way] = send(
                        self.sums.at[chunk, pl.ds(lo, cut)], self.half.at[way], to
                    )
                    continue
                self.flight[way].wait_recv()
                if s == 1:
                    self.sums[chunk, pl.ds(lo, cut)] += self.half[way]
                else:
                    self.sums[chunk] += self.full[way, s - 2]
                self.flight[way] = send(
                    self.sums.at[chunk], self.full.at[way, s - 1], to
                )

        def finish(self):
            for copy in self.flight:
                copy.wait_recv()
            last = self.size // 2 - 2
            return self.sums[self.at] + self.full[0, last] + self.full[1, last]

    ring_z = Ring(sum_z, half_z, full_z, z, NZ, lambda d: device(dz=d + NZ))
    ring_y = Ring(sum_y, half_y, full_y, y, NY, lambda d: device(dy=d + NY))
    ring_x = Ring(sum_x, half_x, full_x, x, NX, lambda d: device(dx=d + NX))

    def spread(part, got, at, size, hop, order=None):
        if order is None:
            order = sorted(range(1, size), key=lambda k: -min(k, size - k))
        return [
            send(part.at[(at + k) % size], got.at[k - 1], hop(k)) for k in order
        ]

    def collect(copies, part, got, at, size):
        for copy in copies:
            copy.wait_recv()
        total = part[at]
        for k in range(size - 1):
            total = total + got[k]
        return total

    fills = (fill_z, fill_y, fill_x)
    for p, ring in enumerate((ring_z, ring_y, ring_x)):
        loads[p].wait()
        pairs[p].wait_recv()
        lax.fori_loop(0, NZ, fills[p], 0)
        ring.step(0)
    ring_z.step(1)
    ring_y.step(1)
    ring_x.step(1)
    ring_z.step(2)
    ring_y.step(2)
    mid_x[...] = ring_x.finish()
    ring_z.step(3)
    ring_y.step(3)

    def start_x(order):
        return spread(mid_x, got_x, z, NZ, lambda k: device(dz=k), order)

    second_x = start_x((3, 5, 2, 6, 1, 7))
    mid_z[...] = ring_z.finish()
    second_x += start_x((4,))
    done_y = ring_y.finish()
    second_z = spread(mid_z, got_z, y, NY, lambda k: device(dy=k))
    for k in range(NX):
        mid_y[k] = done_y[:, k // 2, (k % 2) * 4 : (k % 2) * 4 + 4]
    second_y = spread(mid_y, got_y, x, NX, lambda k: device(dx=k))

    end_x[...] = collect(second_x, mid_x, got_x, z, NZ)
    third_x = spread(end_x, last_x, y, NY, lambda k: device(dy=k))
    end_y[...] = collect(second_y, mid_y, got_y, x, NX)
    third_y = spread(end_y, last_y, z, NZ, lambda k: device(dz=k))
    done_z = collect(second_z, mid_z, got_z, y, NY)
    for k in range(NX):
        end_z[k] = done_z[k // 2, (k % 2) * 4 : (k % 2) * 4 + 4]
    third_z = spread(end_z, last_z, x, NX, lambda k: device(dx=k))

    thirds = (
        (third_z, end_z, last_z, x, NX),
        (third_y, end_y, last_y, z, NZ),
        (third_x, end_x, last_x, y, NY),
    )
    for load in state_loads:
        load.wait()
    for p, third in enumerate(thirds):
        columns = pl.ds(p * LANES, LANES)
        grad_total = collect(*third)
        new_one = beta_one * states[1, :, columns] + (1.0 - beta_one) * grad_total
        new_two = (
            beta_two * states[2, :, columns]
            + (1.0 - beta_two) * grad_total * grad_total
        )
        update = new_one / correct_one / (jnp.sqrt(new_two / correct_two) + epsilon)
        old = states[0, :, columns]
        new_master = old - learn_rate * (update + decay_rate * old)
        packed[0, :, columns] = grad_total
        packed[1, :, columns] = new_master
        packed[2, :, columns] = new_one
        packed[3, :, columns] = new_two
        gathered[z, y, c, p] = new_master.astype(jnp.bfloat16)

    far_first = (4, 3, 5, 2, 6, 1, 7)
    other = device(dc=1)
    mine = gathered.at[z, y, c, 0]
    first_z = [send(mine, mine, device(dz=k)) for k in far_first]
    mine = gathered.at[z, y, c, pl.ds(1, 2)]
    first_y = [send(mine, mine, device(dy=k)) for k in far_first]

    pack = pltpu.make_async_copy(packed, packed_out, pack_sem)
    pack.start()

    def arrived(copy):
        copy.wait_recv()

    for copy in first_z:
        arrived(copy)
    line = gathered.at[:, y, c, 0]
    next_y = [send(line, line, device(dy=k)) for k in far_first]
    send(line, line, other)
    for copy in first_y:
        arrived(copy)
    line = gathered.at[z, :, c, pl.ds(1, 2)]
    next_z = [send(line, line, device(dz=k)) for k in far_first]
    send(line, line, other)
    last = len(taken)
    for k, copy in reversed(list(zip(far_first, next_y))):
        arrived(copy)
        line = gathered.at[:, (y + NY - k) % NY, c, 0]
        send(line, line, other)
    for k, copy in reversed(list(zip(far_first, next_z))):
        arrived(copy)
        line = gathered.at[(z + NZ - k) % NZ, :, c, pl.ds(1, 2)]
        send(line, line, other)
    for copy in taken[last - 1 :] + [taken[last - 1 - len(far_first) - 1]]:
        arrived(copy)
    for copy in taken:
        copy.wait_send()
    pack.wait()
    assert len(taken) == SEMS, len(taken)


def finish(packed, gathered, *refs):
    outs, (states, weights, load_sem, store_sem) = refs[:5], refs[5:]
    first = pltpu.make_async_copy(gathered, weights, load_sem.at[0])
    second = pltpu.make_async_copy(packed, states, load_sem.at[1])
    first.start()
    second.start()
    first.wait()
    stores = [pltpu.make_async_copy(weights, outs[4], store_sem.at[4])]
    stores[0].start()
    second.wait()
    for k in range(4):
        store = pltpu.make_async_copy(states.at[k], outs[k], store_sem.at[k])
        store.start()
        stores.append(store)
    for store in stores:
        store.wait()


def local(grads, master, moment_one, moment_two):
    view = grads.reshape(2, 8, NZ, NY, NC, PARTS, LANES).transpose(0, 2, 3, 4, 5, 1, 6)
    f32, bf16 = jnp.float32, jnp.bfloat16
    block = jax.ShapeDtypeStruct(master.shape, f32)
    block_all = jax.ShapeDtypeStruct((4,) + master.shape, f32)
    weights = jax.ShapeDtypeStruct((NZ, NY, NC, PARTS, 4, LANES), bf16)
    vmem = pl.BlockSpec(memory_space=pltpu.VMEM)
    hbm = pl.BlockSpec(memory_space=pl.ANY)
    packed, gathered = pl.pallas_call(
        kernel,
        out_shape=(block_all, weights),
        in_specs=[hbm] * 4,
        out_specs=(hbm, vmem),
        scratch_shapes=[
            pltpu.VMEM((3,) + master.shape, f32),
            pltpu.VMEM((4,) + master.shape, f32),
            pltpu.VMEM((PARTS, 2, NZ, NY, 8, LANES), bf16),
            pltpu.VMEM((PARTS, 2, NZ, NY, 8, LANES), bf16),
            pltpu.VMEM((NZ, NY, 2, 8, LANES), f32),
            pltpu.VMEM((NY, NZ, 2, 8, LANES), f32),
            pltpu.VMEM((NX, NZ, NY, 4, LANES), f32),
            pltpu.VMEM((2, NY // 2, 2, 8, LANES), f32),
            pltpu.VMEM((2, NZ // 2 - 1, NY, 2, 8, LANES), f32),
            pltpu.VMEM((2, NZ // 2, 2, 8, LANES), f32),
            pltpu.VMEM((2, NY // 2 - 1, NZ, 2, 8, LANES), f32),
            pltpu.VMEM((2, NZ // 2, NY, 4, LANES), f32),
            pltpu.VMEM((2, NX // 2 - 1, NZ, NY, 4, LANES), f32),
            pltpu.VMEM((NY, 2, 8, LANES), f32),
            pltpu.VMEM((NX, NZ, 4, LANES), f32),
            pltpu.VMEM((NZ, NY, 4, LANES), f32),
            pltpu.VMEM((NY - 1, 2, 8, LANES), f32),
            pltpu.VMEM((NX - 1, NZ, 4, LANES), f32),
            pltpu.VMEM((NZ - 1, NY, 4, LANES), f32),
            pltpu.VMEM((NX, 4, LANES), f32),
            pltpu.VMEM((NZ, 4, LANES), f32),
            pltpu.VMEM((NY, 4, LANES), f32),
            pltpu.VMEM((NX - 1, 4, LANES), f32),
            pltpu.VMEM((NZ - 1, 4, LANES), f32),
            pltpu.VMEM((NY - 1, 4, LANES), f32),
            pltpu.SemaphoreType.DMA((3,)),
            pltpu.SemaphoreType.DMA,
            pltpu.SemaphoreType.DMA((PARTS,)),
            pltpu.SemaphoreType.DMA((SEMS,)),
            pltpu.SemaphoreType.DMA((SEMS,)),
        ],
        compiler_params=pltpu.CompilerParams(collective_id=0, has_side_effects=True),
    )(view, master, moment_one, moment_two)
    outs = pl.pallas_call(
        finish,
        out_shape=(block,) * 4 + (weights,),
        in_specs=[hbm] * 2,
        out_specs=(hbm,) * 5,
        scratch_shapes=[
            pltpu.VMEM(block_all.shape, f32),
            pltpu.VMEM(weights.shape, bf16),
            pltpu.SemaphoreType.DMA((2,)),
            pltpu.SemaphoreType.DMA((5,)),
        ],
    )(packed, gathered)
    secondary = outs[4].transpose(4, 0, 1, 2, 3, 5).reshape(master.shape[0], -1)
    return (*outs[:4], secondary)


def solution(mesh):
    return jax.shard_map(
        local,
        mesh=mesh,
        in_specs=(
            P("hst", "local", None, None),
            P("local", "hst"),
            P("local", "hst"),
            P("local", "hst"),
        ),
        out_specs=(
            P("local", "hst"),
            P("local", "hst"),
            P("local", "hst"),
            P("local", "hst"),
            P("local", None),
        ),
        check_vma=False,
    )
```

```python
import functools

import jax
import jax.numpy as jnp
from jax import lax
from jax.experimental import pallas as pl
from jax.experimental.pallas import tpu as pltpu
from jax.sharding import PartitionSpec as P

beta_one = 0.9
beta_two = 0.95
learn_rate = 0.02
decay_rate = 0.1
epsilon = 1e-08
correct_one = 1.0 - (0.9**50) ** 2
correct_two = 1.0 - (0.95**50) ** 2

NX, NY, NZ, NC = 4, 8, 8, 2
PARTS, LANES = 3, 128
MESH = pl.DeviceIdType.MESH
SEMS = 115


def kernel(
    grads,
    master,
    moment_one,
    moment_two,
    packed_out,
    gathered,
    states,
    packed,
    own,
    peer,
    sum_z,
    sum_y,
    sum_x,
    half_z,
    full_z,
    half_y,
    full_y,
    half_x,
    full_x,
    mid_z,
    mid_y,
    mid_x,
    got_z,
    got_y,
    got_x,
    end_z,
    end_y,
    end_x,
    last_z,
    last_y,
    last_x,
    state_sem,
    pack_sem,
    load_sem,
    send_sem,
    recv_sem,
):
    x = lax.axis_index("local")
    h = lax.axis_index("hst")
    z, y, c = h // (NY * NC), (h // NC) % NY, h % NC

    def device(dx=0, dy=0, dz=0, dc=0):
        there = (((z + dz) % NZ) * NY + (y + dy) % NY) * NC + (c + dc) % NC
        return {"hst": there, "local": (x + dx) % NX}

    taken = []

    def send(src, dst, to):
        slot = len(taken)
        copy = pltpu.make_async_remote_copy(
            src_ref=src,
            dst_ref=dst,
            send_sem=send_sem.at[slot],
            recv_sem=recv_sem.at[slot],
            device_id=to,
            device_id_type=MESH,
        )
        copy.start()
        taken.append(copy)
        return copy

    barrier = pltpu.get_barrier_semaphore()
    peers = [device(dc=1)]
    peers += [device(dx=k) for k in (1, NX - 1)]
    peers += [device(dy=k) for k in (1, NY - 1)]
    peers += [device(dz=k) for k in (1, NZ - 1)]
    for to in peers:
        pl.semaphore_signal(barrier, inc=1, device_id=to, device_id_type=MESH)
    loads = []
    for p in range(PARTS):
        load = pltpu.make_async_copy(
            grads.at[:, :, :, c, p], own.at[p], load_sem.at[p]
        )
        load.start()
        loads.append(load)
    state_loads = []
    for k, ref in enumerate((master, moment_one, moment_two)):
        load = pltpu.make_async_copy(ref, states.at[k], state_sem.at[k])
        load.start()
        state_loads.append(load)
    pl.semaphore_wait(barrier, len(peers))

    pairs = [
        send(grads.at[:, :, :, 1 - c, p], peer.at[p], device(dc=1))
        for p in range(PARTS)
    ]

    def pair_sum(p, row, i, j):
        return own[p, row, i, j].astype(jnp.float32) + peer[p, row, i, j].astype(
            jnp.float32
        )

    def fill_z(i, carry):
        for j in range(NY):
            for row in range(2):
                sum_z[i, j, row] = pair_sum(0, row, i, j)
        return carry

    def fill_y(i, carry):
        for j in range(NY):
            for row in range(2):
                sum_y[j, i, row] = pair_sum(1, row, i, j)
        return carry

    def fill_x(i, carry):
        for j in range(NY):
            for row in range(2):
                both = pair_sum(2, row, i, j)
                sum_x[2 * row, i, j] = both[0:4]
                sum_x[2 * row + 1, i, j] = both[4:8]
        return carry

    class Ring:
        def __init__(self, sums, half, full, at, size, hop):
            self.sums, self.half, self.full = sums, half, full
            self.at, self.size, self.hop = at, size, hop
            self.cut = sums.shape[1] // 2
            self.first = [None, None]
            self.flight = [[None, None], [None, None]]

        def chunk(self, way, s):
            away = self.size // 2 - s
            return (self.at + self.size + (away if way == 0 else -away)) % self.size

        def push(self, way, s, sub):
            part = pl.ds(sub * self.cut, self.cut)
            src = self.sums.at[self.chunk(way, s), part]
            to = self.hop(1 if way == 0 else -1)
            if s == 0:
                self.first[way] = send(src, self.half.at[way], to)
            else:
                dst = self.full.at[way, s - 1, part]
                self.flight[way][sub] = send(src, dst, to)

        def start(self):
            for way in range(2):
                self.push(way, 0, way)
            for way in range(2):
                self.push(way, 1, 1 - way)

        def step(self, s):
            for turn in range(2):
                for way in range(2):
                    sub = way if turn else 1 - way
                    part = pl.ds(sub * self.cut, self.cut)
                    if s == 1:
                        if turn == 0:
                            continue
                        self.first[way].wait_recv()
                        got = self.half[way]
                    else:
                        self.flight[way][sub].wait_recv()
                        got = self.full[way, s - 2, part]
                    self.sums[self.chunk(way, s), part] += got
                    self.push(way, s, sub)

        def finish(self):
            for copy in self.flight[0] + self.flight[1]:
                copy.wait_recv()
            last = self.size // 2 - 2
            return self.sums[self.at] + self.full[0, last] + self.full[1, last]

    ring_z = Ring(sum_z, half_z, full_z, z, NZ, lambda d: device(dz=d + NZ))
    ring_y = Ring(sum_y, half_y, full_y, y, NY, lambda d: device(dy=d + NY))
    ring_x = Ring(sum_x, half_x, full_x, x, NX, lambda d: device(dx=d + NX))

    def spread(part, got, at, size, hop, order=None):
        if order is None:
            order = sorted(range(1, size), key=lambda k: -min(k, size - k))
        return [
            send(part.at[(at + k) % size], got.at[k - 1], hop(k)) for k in order
        ]

    def collect(copies, part, got, at, size):
        for copy in copies:
            copy.wait_recv()
        total = part[at]
        for k in range(size - 1):
            total = total + got[k]
        return total

    fills = (fill_z, fill_y, fill_x)
    for p, ring in enumerate((ring_z, ring_y, ring_x)):
        loads[p].wait()
        pairs[p].wait_recv()
        lax.fori_loop(0, NZ, fills[p], 0)
        ring.start()
    ring_z.step(1)
    ring_y.step(1)
    ring_x.step(1)
    ring_z.step(2)
    ring_y.step(2)
    mid_x[...] = ring_x.finish()
    ring_z.step(3)
    ring_y.step(3)

    def start_x(order):
        return spread(mid_x, got_x, z, NZ, lambda k: device(dz=k), order)

    second_x = start_x((3, 5, 2, 6, 1, 7))
    mid_z[...] = ring_z.finish()
    second_x += start_x((4,))
    done_y = ring_y.finish()
    second_z = spread(mid_z, got_z, y, NY, lambda k: device(dy=k))
    for k in range(NX):
        mid_y[k] = done_y[:, k // 2, (k % 2) * 4 : (k % 2) * 4 + 4]
    second_y = spread(mid_y, got_y, x, NX, lambda k: device(dx=k))

    end_x[...] = collect(second_x, mid_x, got_x, z, NZ)
    third_x = spread(end_x, last_x, y, NY, lambda k: device(dy=k))
    end_y[...] = collect(second_y, mid_y, got_y, x, NX)
    third_y = spread(end_y, last_y, z, NZ, lambda k: device(dz=k))
    done_z = collect(second_z, mid_z, got_z, y, NY)
    for k in range(NX):
        end_z[k] = done_z[k // 2, (k % 2) * 4 : (k % 2) * 4 + 4]
    third_z = spread(end_z, last_z, x, NX, lambda k: device(dx=k))

    thirds = (
        (third_z, end_z, last_z, x, NX),
        (third_y, end_y, last_y, z, NZ),
        (third_x, end_x, last_x, y, NY),
    )
    far_first = (4, 3, 5, 2, 6, 1, 7)
    for load in state_loads:
        load.wait()
    for p, third in enumerate(thirds):
        columns = pl.ds(p * LANES, LANES)
        grad_total = collect(*third)
        new_one = beta_one * states[1, :, columns] + (1.0 - beta_one) * grad_total
        new_two = (
            beta_two * states[2, :, columns]
            + (1.0 - beta_two) * grad_total * grad_total
        )
        update = new_one / correct_one / (jnp.sqrt(new_two / correct_two) + epsilon)
        old = states[0, :, columns]
        new_master = old - learn_rate * (update + decay_rate * old)
        packed[0, :, columns] = grad_total
        packed[1, :, columns] = new_master
        packed[2, :, columns] = new_one
        packed[3, :, columns] = new_two
        gathered[z, y, c, p] = new_master.astype(jnp.bfloat16)
        if p == 0:
            mine = gathered.at[z, y, c, 0]
            first_z = [send(mine, mine, device(dz=k)) for k in far_first]

    other = device(dc=1)
    mine = gathered.at[z, y, c, pl.ds(1, 2)]
    first_y = [send(mine, mine, device(dy=k)) for k in far_first]

    pack = pltpu.make_async_copy(packed, packed_out, pack_sem)
    pack.start()

    def arrived(copy):
        copy.wait_recv()

    for copy in first_z:
        arrived(copy)
    line = gathered.at[:, y, c, 0]
    next_y = [send(line, line, device(dy=k)) for k in far_first]
    send(line, line, other)
    for copy in first_y:
        arrived(copy)
    line = gathered.at[z, :, c, pl.ds(1, 2)]
    next_z = [send(line, line, device(dz=k)) for k in far_first]
    send(line, line, other)
    last = len(taken)
    for k, copy in reversed(list(zip(far_first, next_y))):
        arrived(copy)
        line = gathered.at[:, (y + NY - k) % NY, c, 0]
        send(line, line, other)
    for k, copy in reversed(list(zip(far_first, next_z))):
        arrived(copy)
        line = gathered.at[(z + NZ - k) % NZ, :, c, pl.ds(1, 2)]
        send(line, line, other)
    for copy in taken[last - 1 :] + [taken[last - 1 - len(far_first) - 1]]:
        arrived(copy)
    for copy in taken:
        copy.wait_send()
    pack.wait()
    assert len(taken) == SEMS, len(taken)


def finish(packed, gathered, *refs):
    outs, (states, weights, load_sem, store_sem) = refs[:5], refs[5:]
    first = pltpu.make_async_copy(gathered, weights, load_sem.at[0])
    second = pltpu.make_async_copy(packed, states, load_sem.at[1])
    first.start()
    second.start()
    first.wait()
    stores = [pltpu.make_async_copy(weights, outs[4], store_sem.at[4])]
    stores[0].start()
    second.wait()
    for k in range(4):
        store = pltpu.make_async_copy(states.at[k], outs[k], store_sem.at[k])
        store.start()
        stores.append(store)
    for store in stores:
        store.wait()


def local(grads, master, moment_one, moment_two):
    view = grads.reshape(2, 8, NZ, NY, NC, PARTS, LANES).transpose(0, 2, 3, 4, 5, 1, 6)
    f32, bf16 = jnp.float32, jnp.bfloat16
    block = jax.ShapeDtypeStruct(master.shape, f32)
    block_all = jax.ShapeDtypeStruct((4,) + master.shape, f32)
    weights = jax.ShapeDtypeStruct((NZ, NY, NC, PARTS, 4, LANES), bf16)
    vmem = pl.BlockSpec(memory_space=pltpu.VMEM)
    hbm = pl.BlockSpec(memory_space=pl.ANY)
    packed, gathered = pl.pallas_call(
        kernel,
        out_shape=(block_all, weights),
        in_specs=[hbm] * 4,
        out_specs=(hbm, vmem),
        scratch_shapes=[
            pltpu.VMEM((3,) + master.shape, f32),
            pltpu.VMEM((4,) + master.shape, f32),
            pltpu.VMEM((PARTS, 2, NZ, NY, 8, LANES), bf16),
            pltpu.VMEM((PARTS, 2, NZ, NY, 8, LANES), bf16),
            pltpu.VMEM((NZ, NY, 2, 8, LANES), f32),
            pltpu.VMEM((NY, NZ, 2, 8, LANES), f32),
            pltpu.VMEM((NX, NZ, NY, 4, LANES), f32),
            pltpu.VMEM((2, NY // 2, 2, 8, LANES), f32),
            pltpu.VMEM((2, NZ // 2 - 1, NY, 2, 8, LANES), f32),
            pltpu.VMEM((2, NZ // 2, 2, 8, LANES), f32),
            pltpu.VMEM((2, NY // 2 - 1, NZ, 2, 8, LANES), f32),
            pltpu.VMEM((2, NZ // 2, NY, 4, LANES), f32),
            pltpu.VMEM((2, NX // 2 - 1, NZ, NY, 4, LANES), f32),
            pltpu.VMEM((NY, 2, 8, LANES), f32),
            pltpu.VMEM((NX, NZ, 4, LANES), f32),
            pltpu.VMEM((NZ, NY, 4, LANES), f32),
            pltpu.VMEM((NY - 1, 2, 8, LANES), f32),
            pltpu.VMEM((NX - 1, NZ, 4, LANES), f32),
            pltpu.VMEM((NZ - 1, NY, 4, LANES), f32),
            pltpu.VMEM((NX, 4, LANES), f32),
            pltpu.VMEM((NZ, 4, LANES), f32),
            pltpu.VMEM((NY, 4, LANES), f32),
            pltpu.VMEM((NX - 1, 4, LANES), f32),
            pltpu.VMEM((NZ - 1, 4, LANES), f32),
            pltpu.VMEM((NY - 1, 4, LANES), f32),
            pltpu.SemaphoreType.DMA((3,)),
            pltpu.SemaphoreType.DMA,
            pltpu.SemaphoreType.DMA((PARTS,)),
            pltpu.SemaphoreType.DMA((SEMS,)),
            pltpu.SemaphoreType.DMA((SEMS,)),
        ],
        compiler_params=pltpu.CompilerParams(collective_id=0, has_side_effects=True),
    )(view, master, moment_one, moment_two)
    outs = pl.pallas_call(
        finish,
        out_shape=(block,) * 4 + (weights,),
        in_specs=[hbm] * 2,
        out_specs=(hbm,) * 5,
        scratch_shapes=[
            pltpu.VMEM(block_all.shape, f32),
            pltpu.VMEM(weights.shape, bf16),
            pltpu.SemaphoreType.DMA((2,)),
            pltpu.SemaphoreType.DMA((5,)),
        ],
    )(packed, gathered)
    secondary = outs[4].transpose(4, 0, 1, 2, 3, 5).reshape(master.shape[0], -1)
    return (*outs[:4], secondary)


def solution(mesh):
    return jax.shard_map(
        local,
        mesh=mesh,
        in_specs=(
            P("hst", "local", None, None),
            P("local", "hst"),
            P("local", "hst"),
            P("local", "hst"),
        ),
        out_specs=(
            P("local", "hst"),
            P("local", "hst"),
            P("local", "hst"),
            P("local", "hst"),
            P("local", None),
        ),
        check_vma=False,
    )
```

```python
import functools

import jax
import jax.numpy as jnp
from jax import lax
from jax.experimental import pallas as pl
from jax.experimental.pallas import tpu as pltpu
from jax.sharding import PartitionSpec as P

beta_one = 0.9
beta_two = 0.95
learn_rate = 0.02
decay_rate = 0.1
epsilon = 1e-08
correct_one = 1.0 - (0.9**50) ** 2
correct_two = 1.0 - (0.95**50) ** 2

NX, NY, NZ, NC = 4, 8, 8, 2
PARTS, LANES = 3, 128
MESH = pl.DeviceIdType.MESH
SEMS = 115


def kernel(
    grads,
    master,
    moment_one,
    moment_two,
    packed_out,
    gathered,
    states,
    packed,
    own,
    peer,
    sum_z,
    sum_y,
    sum_x,
    half_z,
    full_z,
    half_y,
    full_y,
    half_x,
    full_x,
    mid_z,
    mid_y,
    mid_x,
    got_z,
    got_y,
    got_x,
    end_z,
    end_y,
    end_x,
    last_z,
    last_y,
    last_x,
    state_sem,
    pack_sem,
    load_sem,
    send_sem,
    recv_sem,
):
    x = lax.axis_index("local")
    h = lax.axis_index("hst")
    z, y, c = h // (NY * NC), (h // NC) % NY, h % NC

    def device(dx=0, dy=0, dz=0, dc=0):
        there = (((z + dz) % NZ) * NY + (y + dy) % NY) * NC + (c + dc) % NC
        return {"hst": there, "local": (x + dx) % NX}

    taken = []

    def send(src, dst, to):
        slot = len(taken)
        copy = pltpu.make_async_remote_copy(
            src_ref=src,
            dst_ref=dst,
            send_sem=send_sem.at[slot],
            recv_sem=recv_sem.at[slot],
            device_id=to,
            device_id_type=MESH,
        )
        copy.start()
        taken.append(copy)
        return copy

    barrier = pltpu.get_barrier_semaphore()
    peers = [device(dc=1)]
    peers += [device(dx=k) for k in (1, NX - 1)]
    peers += [device(dy=k) for k in (1, NY - 1)]
    peers += [device(dz=k) for k in (1, NZ - 1)]
    for to in peers:
        pl.semaphore_signal(barrier, inc=1, device_id=to, device_id_type=MESH)
    loads = []
    for p in range(PARTS):
        load = pltpu.make_async_copy(
            grads.at[:, :, :, c, p], own.at[p], load_sem.at[p]
        )
        load.start()
        loads.append(load)
    state_loads = []
    for k, ref in enumerate((master, moment_one, moment_two)):
        load = pltpu.make_async_copy(ref, states.at[k], state_sem.at[k])
        load.start()
        state_loads.append(load)
    pl.semaphore_wait(barrier, len(peers))

    pairs = [
        send(grads.at[:, :, :, 1 - c, p], peer.at[p], device(dc=1))
        for p in range(PARTS)
    ]

    def pair_sum(p, row, i, j):
        return own[p, row, i, j].astype(jnp.float32) + peer[p, row, i, j].astype(
            jnp.float32
        )

    def fill_z(i, carry):
        for j in range(NY):
            for row in range(2):
                sum_z[i, j, row] = pair_sum(0, row, i, j)
        return carry

    def fill_y(i, carry):
        for j in range(NY):
            for row in range(2):
                sum_y[j, i, row] = pair_sum(1, row, i, j)
        return carry

    def fill_x(i, carry):
        for j in range(NY):
            for row in range(2):
                both = pair_sum(2, row, i, j)
                sum_x[2 * row, i, j] = both[0:4]
                sum_x[2 * row + 1, i, j] = both[4:8]
        return carry

    class Ring:
        def __init__(self, sums, half, full, at, size, hop):
            self.sums, self.half, self.full = sums, half, full
            self.at, self.size, self.hop = at, size, hop
            self.cut = sums.shape[1] // 2
            self.first = [None, None]
            self.flight = [[None, None], [None, None]]

        def chunk(self, way, s):
            away = self.size // 2 - s
            return (self.at + self.size + (away if way == 0 else -away)) % self.size

        def push(self, way, s, sub):
            part = pl.ds(sub * self.cut, self.cut)
            src = self.sums.at[self.chunk(way, s), part]
            to = self.hop(1 if way == 0 else -1)
            if s == 0:
                self.first[way] = send(src, self.half.at[way], to)
            else:
                dst = self.full.at[way, s - 1, part]
                self.flight[way][sub] = send(src, dst, to)

        def start(self):
            for way in range(2):
                self.push(way, 0, way)
            for way in range(2):
                self.push(way, 1, 1 - way)

        def step(self, s):
            for turn in range(2):
                for way in range(2):
                    sub = way if turn else 1 - way
                    part = pl.ds(sub * self.cut, self.cut)
                    if s == 1:
                        if turn == 0:
                            continue
                        self.first[way].wait_recv()
                        got = self.half[way]
                    else:
                        self.flight[way][sub].wait_recv()
                        got = self.full[way, s - 2, part]
                    self.sums[self.chunk(way, s), part] += got
                    self.push(way, s, sub)

        def finish(self):
            for copy in self.flight[0] + self.flight[1]:
                copy.wait_recv()
            last = self.size // 2 - 2
            return self.sums[self.at] + self.full[0, last] + self.full[1, last]

    ring_z = Ring(sum_z, half_z, full_z, z, NZ, lambda d: device(dz=d + NZ))
    ring_y = Ring(sum_y, half_y, full_y, y, NY, lambda d: device(dy=d + NY))
    ring_x = Ring(sum_x, half_x, full_x, x, NX, lambda d: device(dx=d + NX))

    def spread(part, got, at, size, hop, order=None):
        if order is None:
            order = sorted(range(1, size), key=lambda k: -min(k, size - k))
        return [
            send(part.at[(at + k) % size], got.at[k - 1], hop(k)) for k in order
        ]

    def collect(copies, part, got, at, size):
        for copy in copies:
            copy.wait_recv()
        total = part[at]
        for k in range(size - 1):
            total = total + got[k]
        return total

    fills = (fill_z, fill_y, fill_x)
    for p, ring in enumerate((ring_z, ring_y, ring_x)):
        loads[p].wait()
        pairs[p].wait_recv()
        lax.fori_loop(0, NZ, fills[p], 0)
        ring.start()
    ring_z.step(1)
    ring_y.step(1)
    ring_x.step(1)
    ring_z.step(2)
    ring_y.step(2)
    mid_x[...] = ring_x.finish()
    ring_z.step(3)
    ring_y.step(3)

    def start_x(order):
        return spread(mid_x, got_x, z, NZ, lambda k: device(dz=k), order)

    second_x = start_x((3, 5, 2, 6, 1, 7))
    mid_z[...] = ring_z.finish()
    second_x += start_x((4,))
    done_y = ring_y.finish()
    second_z = spread(mid_z, got_z, y, NY, lambda k: device(dy=k))
    for k in range(NX):
        mid_y[k] = done_y[:, k // 2, (k % 2) * 4 : (k % 2) * 4 + 4]
    second_y = spread(mid_y, got_y, x, NX, lambda k: device(dx=k))

    end_x[...] = collect(second_x, mid_x, got_x, z, NZ)
    third_x = spread(end_x, last_x, y, NY, lambda k: device(dy=k))
    end_y[...] = collect(second_y, mid_y, got_y, x, NX)
    third_y = spread(end_y, last_y, z, NZ, lambda k: device(dz=k))
    done_z = collect(second_z, mid_z, got_z, y, NY)
    for k in range(NX):
        end_z[k] = done_z[k // 2, (k % 2) * 4 : (k % 2) * 4 + 4]
    third_z = spread(end_z, last_z, x, NX, lambda k: device(dx=k))

    thirds = (
        (third_z, end_z, last_z, x, NX),
        (third_y, end_y, last_y, z, NZ),
        (third_x, end_x, last_x, y, NY),
    )
    far_first = (4, 3, 5, 2, 6, 1, 7)
    for load in state_loads:
        load.wait()
    for p, third in enumerate(thirds):
        columns = pl.ds(p * LANES, LANES)
        grad_total = collect(*third)
        new_one = beta_one * states[1, :, columns] + (1.0 - beta_one) * grad_total
        new_two = (
            beta_two * states[2, :, columns]
            + (1.0 - beta_two) * grad_total * grad_total
        )
        update = new_one / correct_one / (jnp.sqrt(new_two / correct_two) + epsilon)
        old = states[0, :, columns]
        new_master = old - learn_rate * (update + decay_rate * old)
        packed[0, :, columns] = grad_total
        packed[1, :, columns] = new_master
        packed[2, :, columns] = new_one
        packed[3, :, columns] = new_two
        gathered[z, y, c, p] = new_master.astype(jnp.bfloat16)
        if p == 0:
            mine = gathered.at[z, y, c, 0]
            first_z = [send(mine, mine, device(dz=k)) for k in far_first]

    other = device(dc=1)
    mine = gathered.at[z, y, c, pl.ds(1, 2)]
    first_y = [send(mine, mine, device(dy=k)) for k in far_first]

    pack = pltpu.make_async_copy(packed, packed_out, pack_sem)
    pack.start()

    def line_copy(slot, ref, to):
        return pltpu.make_async_remote_copy(
            src_ref=ref,
            dst_ref=ref,
            send_sem=send_sem.at[slot],
            recv_sem=recv_sem.at[slot],
            device_id=to,
            device_id_type=MESH,
        )

    line_y = gathered.at[:, y, c, 0]
    line_z = gathered.at[z, :, c, pl.ds(1, 2)]
    next_y, next_z = [], []
    for nexts, line, hop in (
        (next_y, line_y, lambda k: device(dy=k)),
        (next_z, line_z, lambda k: device(dz=k)),
    ):
        for k in far_first:
            copy = line_copy(len(taken), line, hop(k))
            nexts.append((len(taken), k, copy))
            taken.append(copy)

    def pass_y(k):
        piece = gathered.at[(z + NZ - k) % NZ, y, c, 0]
        for slot, far, _ in next_y:
            line_copy(slot, piece, device(dy=far)).start()

    def pass_z(k):
        piece = gathered.at[z, (y + NY - k) % NY, c, pl.ds(1, 2)]
        for slot, far, _ in next_z:
            line_copy(slot, piece, device(dz=far)).start()

    pass_y(0)
    pass_z(0)
    for k, copy_z, copy_y in reversed(list(zip(far_first, first_z, first_y))):
        copy_z.wait_recv()
        pass_y(k)
        copy_y.wait_recv()
        pass_z(k)
    across = [send(line_y, line_y, other), send(line_z, line_z, other)]
    for (_, k, copy_y), (_, _, copy_z) in reversed(list(zip(next_y, next_z))):
        copy_y.wait_recv()
        line = gathered.at[:, (y + NY - k) % NY, c, 0]
        across.append(send(line, line, other))
        copy_z.wait_recv()
        line = gathered.at[(z + NZ - k) % NZ, :, c, pl.ds(1, 2)]
        across.append(send(line, line, other))
    for copy in across:
        copy.wait_recv()
    for copy in taken:
        copy.wait_send()
    pack.wait()
    assert len(taken) == SEMS, len(taken)


def finish(packed, gathered, *refs):
    outs, (states, weights, load_sem, store_sem) = refs[:5], refs[5:]
    first = pltpu.make_async_copy(gathered, weights, load_sem.at[0])
    second = pltpu.make_async_copy(packed, states, load_sem.at[1])
    first.start()
    second.start()
    first.wait()
    stores = [pltpu.make_async_copy(weights, outs[4], store_sem.at[4])]
    stores[0].start()
    second.wait()
    for k in range(4):
        store = pltpu.make_async_copy(states.at[k], outs[k], store_sem.at[k])
        store.start()
        stores.append(store)
    for store in stores:
        store.wait()


def local(grads, master, moment_one, moment_two):
    view = grads.reshape(2, 8, NZ, NY, NC, PARTS, LANES).transpose(0, 2, 3, 4, 5, 1, 6)
    f32, bf16 = jnp.float32, jnp.bfloat16
    block = jax.ShapeDtypeStruct(master.shape, f32)
    block_all = jax.ShapeDtypeStruct((4,) + master.shape, f32)
    weights = jax.ShapeDtypeStruct((NZ, NY, NC, PARTS, 4, LANES), bf16)
    vmem = pl.BlockSpec(memory_space=pltpu.VMEM)
    hbm = pl.BlockSpec(memory_space=pl.ANY)
    packed, gathered = pl.pallas_call(
        kernel,
        out_shape=(block_all, weights),
        in_specs=[hbm] * 4,
        out_specs=(hbm, vmem),
        scratch_shapes=[
            pltpu.VMEM((3,) + master.shape, f32),
            pltpu.VMEM((4,) + master.shape, f32),
            pltpu.VMEM((PARTS, 2, NZ, NY, 8, LANES), bf16),
            pltpu.VMEM((PARTS, 2, NZ, NY, 8, LANES), bf16),
            pltpu.VMEM((NZ, NY, 2, 8, LANES), f32),
            pltpu.VMEM((NY, NZ, 2, 8, LANES), f32),
            pltpu.VMEM((NX, NZ, NY, 4, LANES), f32),
            pltpu.VMEM((2, NY // 2, 2, 8, LANES), f32),
            pltpu.VMEM((2, NZ // 2 - 1, NY, 2, 8, LANES), f32),
            pltpu.VMEM((2, NZ // 2, 2, 8, LANES), f32),
            pltpu.VMEM((2, NY // 2 - 1, NZ, 2, 8, LANES), f32),
            pltpu.VMEM((2, NZ // 2, NY, 4, LANES), f32),
            pltpu.VMEM((2, NX // 2 - 1, NZ, NY, 4, LANES), f32),
            pltpu.VMEM((NY, 2, 8, LANES), f32),
            pltpu.VMEM((NX, NZ, 4, LANES), f32),
            pltpu.VMEM((NZ, NY, 4, LANES), f32),
            pltpu.VMEM((NY - 1, 2, 8, LANES), f32),
            pltpu.VMEM((NX - 1, NZ, 4, LANES), f32),
            pltpu.VMEM((NZ - 1, NY, 4, LANES), f32),
            pltpu.VMEM((NX, 4, LANES), f32),
            pltpu.VMEM((NZ, 4, LANES), f32),
            pltpu.VMEM((NY, 4, LANES), f32),
            pltpu.VMEM((NX - 1, 4, LANES), f32),
            pltpu.VMEM((NZ - 1, 4, LANES), f32),
            pltpu.VMEM((NY - 1, 4, LANES), f32),
            pltpu.SemaphoreType.DMA((3,)),
            pltpu.SemaphoreType.DMA,
            pltpu.SemaphoreType.DMA((PARTS,)),
            pltpu.SemaphoreType.DMA((SEMS,)),
            pltpu.SemaphoreType.DMA((SEMS,)),
        ],
        compiler_params=pltpu.CompilerParams(collective_id=0, has_side_effects=True),
    )(view, master, moment_one, moment_two)
    outs = pl.pallas_call(
        finish,
        out_shape=(block,) * 4 + (weights,),
        in_specs=[hbm] * 2,
        out_specs=(hbm,) * 5,
        scratch_shapes=[
            pltpu.VMEM(block_all.shape, f32),
            pltpu.VMEM(weights.shape, bf16),
            pltpu.SemaphoreType.DMA((2,)),
            pltpu.SemaphoreType.DMA((5,)),
        ],
    )(packed, gathered)
    secondary = outs[4].transpose(4, 0, 1, 2, 3, 5).reshape(master.shape[0], -1)
    return (*outs[:4], secondary)


def solution(mesh):
    return jax.shard_map(
        local,
        mesh=mesh,
        in_specs=(
            P("hst", "local", None, None),
            P("local", "hst"),
            P("local", "hst"),
            P("local", "hst"),
        ),
        out_specs=(
            P("local", "hst"),
            P("local", "hst"),
            P("local", "hst"),
            P("local", "hst"),
            P("local", None),
        ),
        check_vma=False,
    )
```
